512 devices in a mesh: ctx: 128 (over y, z_hi, x, core), hd: 4 (over z_lo).
Axes of the slice: x: 4, y: 4, z: 16 (z_hi: 4, z_lo: 4; z = z_hi * 4 + z_lo), core: 2. Of those that a mesh axis runs over, the one named last changes fastest.
Arguments:
- cot: bfloat16 [512, 1024], P('ctx'), may hold values from -768 to 768
- resid: bfloat16 [512, 1024], P('ctx'), may hold values from -17 to 17
- norm_gain: bfloat16 [1024], replicated, may hold values from 0.5 to 1.5
- w_in: bfloat16 [1024, 4096], P(None, 'hd'), may hold values from -0.1875 to 0.1875
- w_out: bfloat16 [4096, 1024], P('hd'), may hold values from -0.09375 to 0.09375
- w_proj: bfloat16 [1024, 1024], P('hd', 'ctx'), may hold values from -0.1875 to 0.1875
- queries: bfloat16 [512, 1024], P('ctx', 'hd'), may hold values from -36 to 36
- keys: bfloat16 [32768, 1024], P('ctx', 'hd'), may hold values from -9 to 9
- values: bfloat16 [32768, 1024], P('ctx', 'hd'), may hold values from -6 to 6
- latent_pos: int32 [512], replicated, may hold values from 16384 to 32767, as said below
- seg_start: int32 [512], replicated, may hold values from 16128 to 32766, as said below
Outputs:
- query_grad: bfloat16 [512, 1024], P('ctx', 'hd')
- key_grad: bfloat16 [32768, 1024], P('ctx', 'hd')
- value_grad: bfloat16 [32768, 1024], P('ctx', 'hd')
The draws below stay inside these ranges and needn't reach their ends.
Inputs may be any that keep to these rules, and one draw needn't show every extreme that they name: `latent_pos`: not falling along the latents. seg_start of a latent is 1 to 256 below its latent_pos.
All inputs are finite; a program needn't handle non-finite values.
Results may differ from the reference program's by a relative error of at most 0.012.
Values may be sent and summed in bfloat16 or wider, within the bound.
A program may use at most 64 MiB of HBM per device.

```python
import math
import jax
import jax.numpy as jnp
from jax import lax

D = 1024
HEADS = 16
FF = 4096
HDIM = 64
CTX_DEV = 256
LATENTS = 512
EVENTS = 32768


def positions(key):
    half = EVENTS // 2
    small_gaps = jax.random.randint(jax.random.fold_in(key, 101), (LATENTS - 1,), 1, 3).astype(jnp.int32)
    jump_count = max(1, LATENTS // 64)
    order = jax.random.permutation(jax.random.fold_in(key, 109), LATENTS - 1).astype(jnp.int32)
    chosen = order[:jump_count]
    weights = jax.random.randint(jax.random.fold_in(key, 110), (jump_count,), 1, 101).astype(jnp.int32)
    remaining = (half - 1 - jnp.sum(small_gaps)).astype(jnp.int32)
    shares = (remaining * weights // jnp.sum(weights)).astype(jnp.int32)
    shares = shares.at[jump_count - 1].add(remaining - jnp.sum(shares)).astype(jnp.int32)
    gaps = small_gaps.at[chosen].add(shares).astype(jnp.int32)
    steps_taken = jnp.concatenate([jnp.zeros((1,), jnp.int32), jnp.cumsum(gaps).astype(jnp.int32)])
    return (half + steps_taken).astype(jnp.int32)


def draw_latent_pos(key, part):
    return positions(key)


def draw_seg_start(key, part):
    spots = positions(key)
    latent_index = jnp.arange(LATENTS, dtype=jnp.int32)
    spans = jax.random.randint(jax.random.fold_in(key, 102), (LATENTS,), 1, CTX_DEV + 1).astype(jnp.int32)
    spans = jnp.where(latent_index == 0, CTX_DEV, jnp.where(latent_index == LATENTS - 1, 1, spans))
    return (spots - spans).astype(jnp.int32)


def draw_queries(key, part):
    base = jax.random.truncated_normal(jax.random.fold_in(key, 105), -4.0, 4.0, (LATENTS, D), jnp.float32)
    return base.astype(jnp.bfloat16)


def draw_keys(key, part):
    base = jax.random.truncated_normal(jax.random.fold_in(key, 106), -4.0, 4.0, (EVENTS, D), jnp.float32)
    return base.astype(jnp.bfloat16)


def draw_resid(key, part):
    base = jax.random.truncated_normal(jax.random.fold_in(key, 107), -4.0, 4.0, (LATENTS, D), jnp.float32)
    return base.astype(jnp.bfloat16)


def levels(stream_key, dims, split, low, largest):
    loudness, own = 1.0, jax.random.fold_in(stream_key, 6)
    for position, shards_of in split:
        heights = jnp.exp(jax.random.uniform(jax.random.fold_in(own, position), (shards_of,), jnp.float32, low / len(split), largest / len(split)))
        loudness = loudness * jnp.repeat(heights, dims[position] // shards_of).reshape([-1 if axis == position else 1 for axis in range(len(dims))])
    return loudness


def bell_draw(own_key, shape, scale, most, shards=(), kind=jnp.bfloat16):
    entries = jax.random.normal(own_key, shape, jnp.float32) * scale
    if len(shards) > 0:
        entries = levels(own_key, shape, shards, -0.22, 0.18) * entries
    return jnp.clip(entries, min=-most, max=most).astype(kind)


def setup_inputs(seed: int = 0) -> dict:
    seeds = jax.random.split(jax.random.key(seed), 12)
    return {
        "cot": bell_draw(seeds[0], (LATENTS, D), 128.0, 768.0, ((0, 128),)),
        "resid": draw_resid(jax.random.fold_in(seeds[11], 71), 0),
        "norm_gain": jnp.clip(1.0 + 0.1 * jax.random.normal(seeds[2], (D,), jnp.float32), 0.5, 1.5).astype(jnp.bfloat16),
        "w_in": bell_draw(seeds[3], (D, FF), D ** -0.5, 0.1875, ((1, 4),)),
        "w_out": bell_draw(seeds[4], (FF, D), FF ** -0.5, 0.09375, ((0, 4),)),
        "w_proj": bell_draw(seeds[5], (D, D), D ** -0.5, 0.1875, ((0, 4), (1, 128))),
        "queries": draw_queries(jax.random.fold_in(seeds[11], 71), 0),
        "keys": draw_keys(jax.random.fold_in(seeds[11], 71), 0),
        "values": bell_draw(seeds[8], (EVENTS, D), 1.0, 6.0, ((0, 128), (1, 4))),
        "latent_pos": draw_latent_pos(jax.random.fold_in(seeds[11], 71), 0),
        "seg_start": draw_seg_start(jax.random.fold_in(seeds[11], 71), 0),
    }


def gelu_slope(values_in):
    inner = 0.7978845608028654 * (values_in + 0.044715 * values_in * values_in * values_in)
    tangent = jnp.tanh(inner)
    return 0.5 * (1.0 + tangent) + 0.5 * values_in * (1.0 - tangent * tangent) * 0.7978845608028654 * (1.0 + 0.134145 * values_in * values_in)

def split_heads(array):
    return array.reshape(array.shape[0], HEADS, HDIM).transpose(1, 0, 2)

def join_heads(array):
    return array.transpose(1, 0, 2).reshape(array.shape[1], HEADS * HDIM)

def reference(cot, resid, norm_gain, w_in, w_out, w_proj, queries, keys, values, latent_pos, seg_start):
    rows_f32 = resid.astype(jnp.float32)
    inv_rms = lax.rsqrt(lax.optimization_barrier(jnp.mean(rows_f32 * rows_f32, axis=-1, keepdims=True)) + 1e-05)
    gain_f32 = norm_gain.astype(jnp.float32)
    normed = (rows_f32 * inv_rms * gain_f32).astype(jnp.bfloat16)
    pre_act = jnp.dot(normed, w_in, preferred_element_type=jnp.float32)
    hidden_grad = jnp.dot(cot, w_out.T, preferred_element_type=jnp.float32)
    pre_grad = (hidden_grad * gelu_slope(pre_act)).astype(jnp.bfloat16)
    normed_grad = jnp.dot(pre_grad, w_in.T, preferred_element_type=jnp.float32)
    weighted = normed_grad * gain_f32
    unit_rows = rows_f32 * inv_rms
    resid_grad = (cot.astype(jnp.float32) + inv_rms * (weighted - unit_rows * lax.optimization_barrier(jnp.mean(weighted * unit_rows, axis=-1, keepdims=True)))).astype(jnp.bfloat16)
    out_grad = jnp.dot(resid_grad, w_proj.T, preferred_element_type=jnp.float32).astype(jnp.bfloat16)
    latents = queries.shape[0]
    events = keys.shape[0]
    event_index = jnp.arange(events, dtype=jnp.int32)
    block_rows = min(latents, 512)
    blocks = latents // block_rows
    factor = 1.0 / math.sqrt(HDIM)

    def one_head(inputs):
        head_q, head_k, head_v, head_do = inputs

        def one_block(carry, block_in):
            key_acc, value_acc = carry
            block_q, block_do, block_pos, block_start = block_in
            scores = factor * jnp.dot(block_q, head_k.T, preferred_element_type=jnp.float32)
            visible = (event_index[None, :] >= block_start[:, None]) & (event_index[None, :] <= block_pos[:, None])
            top = lax.optimization_barrier(jnp.max(jnp.where(visible, scores, -1e+30), axis=1, keepdims=True))
            expo = jnp.where(visible, jnp.exp(scores - top), 0.0)
            probs = expo / lax.optimization_barrier(jnp.sum(expo, axis=1, keepdims=True))
            prob_grad = jnp.dot(block_do, head_v.T, preferred_element_type=jnp.float32)
            delta = lax.optimization_barrier(jnp.sum(probs * prob_grad, axis=1, keepdims=True))
            prob_round = probs.astype(jnp.bfloat16)
            score_grad = (factor * probs * (prob_grad - delta)).astype(jnp.bfloat16)
            value_acc = value_acc + jnp.dot(prob_round.T, block_do, preferred_element_type=jnp.float32)
            key_acc = key_acc + jnp.dot(score_grad.T, block_q, preferred_element_type=jnp.float32)
            query_block = jnp.dot(score_grad, head_k, preferred_element_type=jnp.float32).astype(jnp.bfloat16)
            return ((key_acc, value_acc), query_block)
        block_inputs = (head_q.reshape(blocks, block_rows, HDIM), head_do.reshape(blocks, block_rows, HDIM), latent_pos.reshape(blocks, block_rows), seg_start.reshape(blocks, block_rows))
        start_acc = (jnp.zeros((events, HDIM), jnp.float32), jnp.zeros((events, HDIM), jnp.float32))
        (key_acc, value_acc), query_blocks = lax.scan(one_block, start_acc, block_inputs)
        return (query_blocks.reshape(latents, HDIM), key_acc.astype(jnp.bfloat16), value_acc.astype(jnp.bfloat16))
    query_heads, key_heads, value_heads = lax.map(one_head, (split_heads(queries), split_heads(keys), split_heads(values), split_heads(out_grad)))
    return (join_heads(query_heads), join_heads(key_heads), join_heads(value_heads))
```

```python
import jax
import jax.numpy as jnp
from jax import lax
from jax.experimental import pallas as pl
from jax.experimental.pallas import tpu as pltpu
from jax.sharding import PartitionSpec as P

F32, BF16 = jnp.float32, jnp.bfloat16
MESH = pl.DeviceIdType.MESH
D = 1024
HID = 1024
FEAT = 256
HDIM = 64
HEADS = 4
EV = 256
LAT = 512
CTX_COUNT = 128
FIRST_EVENTS = 63
WIDE = 384
SENDS = 136
EMPTY = -1e29
NN = (((1,), (0,)), ((), ()))
NT = (((1,), (1,)), ((), ()))


def gelu_slope(t):
    inner = 0.7978845608028654 * (t + 0.044715 * t * t * t)
    tangent = jnp.tanh(inner)
    return 0.5 * (1.0 + tangent) + 0.5 * t * (
        1.0 - tangent * tangent
    ) * 0.7978845608028654 * (1.0 + 0.134145 * t * t)


def dot(a, b, dims=NN):
    return lax.dot_general(a, b, dims, preferred_element_type=F32)


def pieces(stats):
    high = stats.astype(BF16).astype(F32)
    rest = stats - high
    middle = rest.astype(BF16).astype(F32)
    return high, middle, rest - middle


def lanes_of(rows, columns, width):
    lane = lax.broadcasted_iota(jnp.int32, (rows, columns), 0)
    to = lax.broadcasted_iota(jnp.int32, (rows, columns), 1)
    same = ((lane & 3) == ((to >> 6) & 3)) & (((lane >> 2) & 1) == (to >> 8))
    return jnp.where(same & (lane < width), 1.0, 0.0).astype(BF16)


def wide_rows(main, stats):
    tail = jnp.concatenate(
        [*pieces(stats), jnp.zeros((WIDE - FEAT - 24, LAT), F32)], axis=0
    )
    return jnp.concatenate([main, tail], axis=0).T.astype(BF16).reshape(32, 16, WIDE)


def shares(tops, totals):
    top = tops[0]
    for n in range(1, len(tops)):
        top = jnp.maximum(top, tops[n])
    parts = [total * jnp.exp(own - top) for own, total in zip(tops, totals)]
    whole = parts[0]
    for n in range(1, len(tops)):
        whole = whole + parts[n]
    scale = jnp.where(whole > 0.0, 1.0 / whole, 0.0)
    return top, whole, [part * scale for part in parts]


def added(terms):
    whole = terms[0]
    for term in terms[1:]:
        whole = whole + term
    return whole


def kernel(
    cot_h, res_h, gain_h, win_h, wout_h, wt_h, q_h, k_h, v_h, pos_h, start_h,
    oq_h, ok_h, ov_h,
    cot_v, res_v, gain_v, win_v, wout_v, wslab, q_v, kbuf, vbuf, pos_v,
    part_s, hdbuf, zw, wfull, qz, qblk, qbuf, rgz, rgall, dosend, dobuf,
    kmask, vmask, kt, bias, pown, gown, near_s, near_r,
    early_s, early_r, late_s, late_r, early_zs, early_zr, late_zs, late_zr,
    dk_v, dv_v, oq_v,
    lsem, ssem, hd_sem, zw_sem, qz_sem, near_sem, w_sem, q_sem, rgz_sem, rgp_sem,
    do_sem, early_sem, late_sem, early_z_sem, late_z_sem, out_sem,
):
    c = lax.axis_index("ctx")
    hd = lax.axis_index("hd")
    core = c % 2
    x = (c // 2) % 4
    zh = (c // 8) % 4
    y = c // 32
    chip = y * 4 + x
    slot = chip * 2 + core
    active = y >= 2
    edge = c == FIRST_EVENTS
    takes_part = c >= FIRST_EVENTS

    def ctx_of(y_, zh_, x_, core_):
        return ((y_ * 4 + zh_) * 4 + x_) * 2 + core_

    barrier = pltpu.get_barrier_semaphore()
    greeted = []
    for d in (4, 5, 2, 3, 6, 7, 1):
        other = (zh * 2 + core + d) % 8
        greeted.append((ctx_of(y, other // 2, x, other % 2), hd))
    for d in range(1, 4):
        greeted.append((c, (hd + d) % 4))
    greeted.append(((c + 1) % CTX_COUNT, hd))
    greeted.append(((c + CTX_COUNT - 1) % CTX_COUNT, hd))
    for d in range(1, 32):
        other = (slot + d) % 32
        greeted.append((ctx_of(other // 8, zh, (other // 2) % 4, other % 2), hd))
    for who in greeted:
        pl.semaphore_signal(barrier, inc=1, device_id=who, device_id_type=MESH)

    loads = {}

    def load(name, src, dst, k):
        copy = pltpu.make_async_copy(src, dst, lsem.at[k])
        copy.start()
        loads[name] = copy

    load("res", res_h, res_v, 0)
    load("cot", cot_h, cot_v, 1)
    load("gain", gain_h, gain_v, 2)
    for n in range(4):
        load(f"win{n}", win_h.at[pl.ds(256 * n, 256)], win_v.at[pl.ds(256 * n, 256)], 3 + n)
    for n in range(4):
        load(f"wout{n}", wout_h.at[pl.ds(256 * n, 256)], wout_v.at[pl.ds(256 * n, 256)], 7 + n)
    load("wt", wt_h, wslab, 11)
    load("q", q_h, q_v, 12)
    load("k", k_h, kbuf, 13)
    load("v", v_h, vbuf, 14)
    load("start", start_h, pos_v.at[0], 15)
    load("pos", pos_h, pos_v.at[1], 16)

    sends = []

    def send(src, dst, recv_sem, who, cond=None):
        copy = pltpu.make_async_remote_copy(
            src_ref=src, dst_ref=dst, send_sem=ssem.at[len(sends)], recv_sem=recv_sem,
            device_id=who, device_id_type=MESH,
        )
        sends.append((cond, copy))
        if cond is None:
            copy.start()
        else:
            pl.when(cond)(copy.start)

    def arrived(ref, sem):
        pltpu.make_async_copy(ref, ref, sem).wait()

    loads["res"].wait()
    loads["gain"].wait()
    loads["cot"].wait()
    rows = res_v[...].astype(F32)
    inv_rms = lax.rsqrt(jnp.mean(rows * rows, axis=-1, keepdims=True) + 1e-05)
    gain_rows = gain_v[...].astype(F32)
    gain = jnp.concatenate([gain_rows[n : n + 1, :] for n in range(8)], axis=1)
    normed = (rows * inv_rms * gain).astype(BF16)
    cot = cot_v[...]
    pre = jnp.zeros((4, HID), F32)
    for n in range(4):
        loads[f"win{n}"].wait()
        pre = pre + dot(normed[:, 256 * n : 256 * n + 256], win_v[256 * n : 256 * n + 256, :])
    slope = gelu_slope(pre)
    hidden = []
    for n in range(4):
        loads[f"wout{n}"].wait()
        hidden.append(dot(cot, wout_v[256 * n : 256 * n + 256, :], NT))
    pre_grad = (jnp.concatenate(hidden, axis=1) * slope).astype(BF16)
    part = dot(pre_grad, win_v[...], NT)
    part_s[...] = part

    loads["wt"].wait()
    loads["q"].wait()
    loads["k"].wait()
    loads["v"].wait()
    loads["pos"].wait()
    loads["start"].wait()
    pl.semaphore_wait(barrier, len(greeted))

    for d in range(1, 4):
        send(part_s, hdbuf.at[hd], hd_sem, (c, (hd + d) % 4))
    for d in range(1, 8):
        other = (zh * 2 + core + d) % 8
        send(
            wslab.at[other % 2], zw.at[zh * 2 + core], zw_sem,
            (ctx_of(y, other // 2, x, other % 2), hd),
        )
    for d in range(1, 4):
        send(q_v, qz.at[zh], qz_sem, (ctx_of(y, (zh + d) % 4, x, core), hd))
    hdbuf[hd] = part
    zw[zh * 2 + core] = wslab[core]
    qz[zh] = q_v[...]

    @pl.when(jnp.logical_not(takes_part))
    def _():
        dk_v[...] = jnp.zeros_like(dk_v)
        dv_v[...] = jnp.zeros_like(dv_v)

    @pl.when(takes_part)
    def _():
        base = c * EV
        spots = jnp.concatenate([pos_v[0], pos_v[1]], axis=0) - base
        to = lax.broadcasted_iota(jnp.int32, (128, 128), 1)
        origin = ((to >> 2) & 3) * 32 + (to >> 5) * 8 + ((to >> 4) & 1) * 4 + (to & 3)
        pick = jnp.where(lax.broadcasted_iota(jnp.int32, (128, 128), 0) == origin, 1.0, 0.0)
        moved = lax.dot_general(
            spots.astype(F32), pick, NN,
            precision=lax.Precision.HIGHEST, preferred_element_type=F32,
        )
        start = jnp.concatenate([moved[n : n + 1, :] for n in range(4)], axis=1)
        stop = jnp.concatenate([moved[n : n + 1, :] for n in range(4, 8)], axis=1)
        event = lax.broadcasted_iota(jnp.int32, (EV, LAT), 0).astype(F32)
        seen = (event >= start) & (event <= stop)
        bias[...] = jnp.where(seen, 0.0, -1e30)
        lane_head = lax.broadcasted_iota(jnp.int32, (1, FEAT), 1) // HDIM
        keys = kbuf[...].astype(F32) * 0.125
        values = vbuf[...].astype(F32)
        kt[...] = keys.T.astype(BF16)
        for h in range(HEADS):
            kmask[h] = jnp.where(lane_head == h, keys, 0.0).astype(BF16)
            vmask[h] = jnp.where(lane_head == h, values, 0.0).astype(BF16)

    arrived(hdbuf.at[0:3], hd_sem)
    normed_grad = (hdbuf[0] + hdbuf[1]) + (hdbuf[2] + hdbuf[3])
    weighted = normed_grad * gain
    unit = rows * inv_rms
    resid_grad = (
        cot.astype(F32)
        + inv_rms * (weighted - unit * jnp.mean(weighted * unit, axis=-1, keepdims=True))
    ).astype(BF16)
    rgz[zh] = resid_grad
    for d in range(1, 4):
        send(rgz.at[zh], rgz.at[zh], rgz_sem, (ctx_of(y, (zh + d) % 4, x, core), hd))

    arrived(zw.at[0:7], zw_sem)
    for j in range(4):
        both = jnp.concatenate([zw[2 * j].astype(F32), zw[2 * j + 1].astype(F32)], axis=0)
        wfull[y, j, x] = both.astype(BF16)
    for d in range(1, 16):
        other = (chip + d) % 16
        send(
            wfull.at[y, :, x], wfull.at[y, :, x], w_sem.at[chip],
            (ctx_of(other // 4, zh, other % 4, core), hd),
        )

    arrived(qz.at[0:3], qz_sem)
    qblk[...] = jnp.concatenate([qz[j].astype(F32) for j in range(4)], axis=0).astype(BF16)

    def to_holders(src, dst, sem):
        for d in range(16):
            t = (slot + d) % 16
            who = ctx_of(2 + t // 8, zh, (t // 2) % 4, t % 2)
            send(src, dst, sem, (who, hd), who != c)
        send(src, dst, sem, (FIRST_EVENTS, hd), (zh == 3) & (c != FIRST_EVENTS))

    to_holders(qblk, qbuf.at[slot], q_sem)

    arrived(rgz.at[0:3], rgz_sem)
    rgall[core] = jnp.concatenate([rgz[j].astype(F32) for j in range(4)], axis=0).astype(BF16)
    send(rgall.at[core], rgall.at[core], rgp_sem, (ctx_of(y, zh, x, 1 - core), hd))

    @pl.when(takes_part)
    def _():
        qbuf[slot] = qblk[...]

    for d in range(1, 16):
        other = (chip + d) % 16
        arrived(wfull.at[other // 4, :, other % 4], w_sem.at[other])
    arrived(rgall.at[1 - core], rgp_sem)
    out_half = dot(rgall[...].reshape(32, D), wfull[...].reshape(D, 128)).astype(BF16)
    dosend[...] = out_half
    to_holders(dosend, dobuf.at[core * 16 + chip], do_sem)

    @pl.when(takes_part)
    def _():
        dobuf[core * 16 + chip] = dosend[...]

    @pl.when(takes_part)
    def _():
        arrived(qbuf.at[0:31], q_sem)

    @pl.when(takes_part)
    def _():
        tops, totals, mixed = [], [], []
        for h in range(HEADS):
            scores = dot(kmask[h], qbuf[...].reshape(LAT, FEAT), NT) + bias[...]
            top = jnp.maximum(jnp.max(scores, axis=0, keepdims=True), EMPTY)
            expo = jnp.exp(scores - top)
            total = jnp.sum(expo, axis=0, keepdims=True)
            probs = expo * jnp.where(total > 0.0, 1.0 / total, 0.0)
            pown[h] = probs
            mixed.append(dot(kt[h * HDIM : (h + 1) * HDIM, :], probs.astype(BF16)))
            tops.append(top)
            totals.append(total)
        stats = jnp.concatenate(tops + totals, axis=0)
        near_s[0:8, :] = stats
        early_s[...] = wide_rows(jnp.concatenate(mixed, axis=0), stats)

    my_turn = jnp.where(active, (y - 2) * 8 + x * 2 + core, 16)

    def to_owners(src, dst, sem):
        for d in range(1, 32):
            s = (slot + d) % 32
            send(
                src.at[s], dst.at[my_turn], sem.at[my_turn],
                (ctx_of(s // 8, zh, (s // 2) % 4, s % 2), hd), takes_part,
            )

    def from_holders(buf, sem):
        for t in range(16):
            who = ctx_of(2 + t // 8, zh, (t // 2) % 4, t % 2)

            @pl.when(who != c)
            def _():
                arrived(buf.at[t], sem.at[t])

        @pl.when((zh == 3) & (c != FIRST_EVENTS))
        def _():
            arrived(buf.at[16], sem.at[16])

    to_owners(early_s, early_r, early_sem)

    @pl.when(takes_part)
    def _():
        early_r[my_turn] = early_s[slot]

    @pl.when(zh != 3)
    def _():
        lane = lax.broadcasted_iota(jnp.int32, (16, WIDE), 1)
        early_r[16] = jnp.where((lane >> 2) == (FEAT >> 2), EMPTY, 0.0).astype(BF16)
        late_r[16] = jnp.zeros((16, WIDE), BF16)

    @pl.when(takes_part)
    def _():
        arrived(dobuf.at[0:31], do_sem)

    def all_grads():
        return jnp.concatenate(
            [dobuf[0:16].reshape(LAT, 128), dobuf[16:32].reshape(LAT, 128)], axis=1
        )

    @pl.when(takes_part)
    def _():
        grads_t = all_grads().astype(F32).T.astype(BF16)
        deltas, mixed = [], []
        for h in range(HEADS):
            prob_grad = dot(vmask[h], grads_t)
            gown[h] = prob_grad
            probs = pown[h]
            delta = jnp.sum(probs * prob_grad, axis=0, keepdims=True)
            score_grad = (probs * (prob_grad - delta)).astype(BF16)
            mixed.append(dot(kt[h * HDIM : (h + 1) * HDIM, :], score_grad))
            deltas.append(delta)
        stats = jnp.concatenate(deltas + [jnp.zeros((4, LAT), F32)], axis=0)
        near_s[8:16, :] = stats
        late_s[...] = wide_rows(jnp.concatenate(mixed, axis=0), stats)

    to_owners(late_s, late_r, late_sem)
    up = takes_part & (c < CTX_COUNT - 1)
    down = c > FIRST_EVENTS
    send(near_s, near_r.at[0], near_sem.at[0], ((c + 1) % CTX_COUNT, hd), up)
    send(near_s, near_r.at[1], near_sem.at[1], ((c + CTX_COUNT - 1) % CTX_COUNT, hd), down)

    @pl.when(takes_part)
    def _():
        late_r[my_turn] = late_s[slot]

    from_holders(early_r, early_sem)
    early = early_r[...].reshape(17 * 16, WIDE)
    spread = dot(early[:, FEAT:], lanes_of(WIDE - FEAT, 2 * FEAT, 24))
    tops = [spread[16 * n : 16 * n + 16, 0:FEAT] for n in range(17)]
    totals = [spread[16 * n : 16 * n + 16, FEAT:] for n in range(17)]
    top, whole, weights = shares(tops, totals)
    mean_keys = [early[16 * n : 16 * n + 16, 0:FEAT].astype(F32) for n in range(17)]
    mean_key = added([w * k for w, k in zip(weights, mean_keys)])
    for j in range(4):
        for k, part_ in enumerate((top, whole, mean_key)):
            early_zs[j, :, k * FEAT : (k + 1) * FEAT] = part_[4 * j : 4 * j + 4, :]
    for d in range(1, 4):
        other = (zh + d) % 4
        send(early_zs.at[other], early_zr.at[zh], early_z_sem, (ctx_of(y, other, x, core), hd))
    early_zr[zh] = early_zs[zh]

    from_holders(late_r, late_sem)
    late = late_r[...].reshape(17 * 16, WIDE)
    spread = dot(late[:, FEAT:], lanes_of(WIDE - FEAT, FEAT, 24))
    deltas = [spread[16 * n : 16 * n + 16, :] for n in range(17)]
    delta = added([w * own for w, own in zip(weights, deltas)])
    merged = added([
        weights[n]
        * (late[16 * n : 16 * n + 16, 0:FEAT].astype(F32) - (delta - deltas[n]) * mean_keys[n])
        for n in range(17)
    ])
    lane = lax.broadcasted_iota(jnp.int32, (FEAT, WIDE - FEAT), 0)
    to = lax.broadcasted_iota(jnp.int32, (FEAT, WIDE - FEAT), 1)
    compact = added([
        dot(
            piece.astype(BF16),
            jnp.where(((lane & 63) == 0) & (to == k * 8 + (lane >> 6)), 1.0, 0.0).astype(BF16),
        )
        for k, piece in enumerate(pieces(delta))
    ])
    for j in range(4):
        late_zs[j, :, 0:FEAT] = merged[4 * j : 4 * j + 4, :].astype(BF16)
        late_zs[j, :, FEAT:] = compact[4 * j : 4 * j + 4, :].astype(BF16)
    for d in range(1, 4):
        other = (zh + d) % 4
        send(late_zs.at[other], late_zr.at[zh], late_z_sem, (ctx_of(y, other, x, core), hd))
    late_zr[zh] = late_zs[zh]

    @pl.when(takes_part)
    def _():
        nothing = jnp.concatenate(
            [jnp.full((4, LAT), EMPTY, F32), jnp.zeros((12, LAT), F32)], axis=0
        )

        @pl.when(c == FIRST_EVENTS)
        def _():
            near_r[0] = nothing

        @pl.when(c == CTX_COUNT - 1)
        def _():
            near_r[1] = nothing

        @pl.when(c > FIRST_EVENTS)
        def _():
            arrived(near_r.at[0], near_sem.at[0])

        @pl.when(c < CTX_COUNT - 1)
        def _():
            arrived(near_r.at[1], near_sem.at[1])

    @pl.when(takes_part)
    def _():
        three = (near_s[...], near_r[0], near_r[1])
        unused_top, unused_whole, parts = shares(
            [one[0:4, :] for one in three], [one[4:8, :] for one in three]
        )
        delta = added([w * one[8:12, :] for w, one in zip(parts, three)])
        queries = qbuf[...].reshape(LAT, FEAT)
        grads = all_grads()
        lane_head = lax.broadcasted_iota(jnp.int32, (1, FEAT), 1) // HDIM
        dk = jnp.zeros((EV, FEAT), F32)
        dv = jnp.zeros((EV, FEAT), F32)
        for h in range(HEADS):
            probs = pown[h] * parts[0][h : h + 1, :]
            score_grad = (probs * (gown[h] - delta[h : h + 1, :])).astype(BF16)
            dk = jnp.where(lane_head == h, dot(score_grad, queries), dk)
            dv = jnp.where(lane_head == h, dot(probs.astype(BF16), grads), dv)
        dk_v[...] = (dk * 0.125).astype(BF16)
        dv_v[...] = dv.astype(BF16)

    out_k = pltpu.make_async_copy(dk_v, ok_h, out_sem.at[0])
    out_v = pltpu.make_async_copy(dv_v, ov_h, out_sem.at[1])
    out_k.start()
    out_v.start()

    arrived(early_zr.at[0:3], early_z_sem)
    tops = [early_zr[j][:, 0:FEAT] for j in range(4)]
    totals = [early_zr[j][:, FEAT : 2 * FEAT] for j in range(4)]
    mean_keys = [early_zr[j][:, 2 * FEAT :] for j in range(4)]
    unused_top, unused_whole, weights = shares(tops, totals)
    arrived(late_zr.at[0:3], late_z_sem)
    late = [late_zr[j].astype(F32) for j in range(4)]
    spread = dot(
        jnp.concatenate([one[:, FEAT:] for one in late], axis=0).astype(BF16),
        lanes_of(WIDE - FEAT, FEAT, 24),
    )
    deltas = [spread[4 * j : 4 * j + 4, :] for j in range(4)]
    delta = added([w * own for w, own in zip(weights, deltas)])
    total = added([
        weights[j] * (late[j][:, 0:FEAT] - (delta - deltas[j]) * mean_keys[j]) for j in range(4)
    ])
    oq_v[...] = total.astype(BF16)
    assert len(sends) == SENDS
    out_q = pltpu.make_async_copy(oq_v, oq_h, out_sem.at[2])
    out_q.start()
    for cond, copy in sends:
        if cond is None:
            copy.wait_send()
        else:
            pl.when(cond)(copy.wait_send)
    out_k.wait()
    out_v.wait()
    out_q.wait()


def put(q_in, k_in, v_in, q_out, k_out, v_out, q_v, k_v, v_v, sem_in, sem_out):
    first = [
        pltpu.make_async_copy(src, dst, sem_in.at[n])
        for n, (src, dst) in enumerate(((k_in, k_v), (v_in, v_v), (q_in, q_v)))
    ]
    second = [
        pltpu.make_async_copy(src, dst, sem_out.at[n])
        for n, (src, dst) in enumerate(((k_v, k_out), (v_v, v_out), (q_v, q_out)))
    ]
    for copy in first:
        copy.start()
    for copy, following in zip(first, second):
        copy.wait()
        following.start()
    for copy in second:
        copy.wait()


def per_device(
    cot, resid, norm_gain, w_in, w_out, w_proj, queries, keys, values, latent_pos, seg_start
):
    w_halves = w_proj.reshape(2, 128, 8).transpose(0, 2, 1)
    anywhere = pl.BlockSpec(memory_space=pl.ANY)
    dma = pltpu.SemaphoreType.DMA
    vm = pltpu.VMEM
    shapes = (
        jax.ShapeDtypeStruct((4, FEAT), BF16),
        jax.ShapeDtypeStruct((EV, FEAT), BF16),
        jax.ShapeDtypeStruct((EV, FEAT), BF16),
    )
    found = pl.pallas_call(
        kernel,
        out_shape=shapes,
        in_specs=[anywhere] * 11,
        out_specs=(anywhere,) * 3,
        scratch_shapes=[
            vm((4, D), BF16),
            vm((4, D), BF16),
            vm((8, 128), BF16),
            vm((D, HID), BF16),
            vm((HID, D), BF16),
            vm((2, 8, 128), BF16),
            vm((4, FEAT), BF16),
            vm((EV, FEAT), BF16),
            vm((EV, FEAT), BF16),
            vm((2, 4, 128), jnp.int32),
            vm((4, D), F32),
            vm((4, 4, D), F32),
            vm((8, 8, 128), BF16),
            vm((4, 4, 4, 16, 128), BF16),
            vm((4, 4, FEAT), BF16),
            vm((16, FEAT), BF16),
            vm((32, 16, FEAT), BF16),
            vm((4, 4, D), BF16),
            vm((2, 16, D), BF16),
            vm((32, 128), BF16),
            vm((32, 32, 128), BF16),
            vm((HEADS, EV, FEAT), BF16),
            vm((HEADS, EV, FEAT), BF16),
            vm((FEAT, EV), BF16),
            vm((EV, LAT), F32),
            vm((HEADS, EV, LAT), F32),
            vm((HEADS, EV, LAT), F32),
            vm((16, LAT), F32),
            vm((2, 16, LAT), F32),
            vm((32, 16, WIDE), BF16),
            vm((17, 16, WIDE), BF16),
            vm((32, 16, WIDE), BF16),
            vm((17, 16, WIDE), BF16),
            vm((4, 4, 3 * FEAT), F32),
            vm((4, 4, 3 * FEAT), F32),
            vm((4, 4, WIDE), BF16),
            vm((4, 4, WIDE), BF16),
            vm((EV, FEAT), BF16),
            vm((EV, FEAT), BF16),
            vm((4, FEAT), BF16),
            dma((17,)),
            dma((SENDS,)),
            dma, dma, dma,
            dma((2,)),
            dma((16,)),
            dma, dma, dma, dma,
            dma((17,)),
            dma((17,)),
            dma, dma,
            dma((3,)),
        ],
        compiler_params=pltpu.CompilerParams(collective_id=0, has_side_effects=True),
        name="backward",
    )(
        cot, resid, norm_gain.reshape(8, 128), w_in, w_out, w_halves, queries, keys, values,
        latent_pos.reshape(4, 128), seg_start.reshape(4, 128),
    )
    return pl.pallas_call(
        put,
        out_shape=shapes,
        in_specs=[anywhere] * 3,
        out_specs=(anywhere,) * 3,
        scratch_shapes=[
            vm((4, FEAT), BF16), vm((EV, FEAT), BF16), vm((EV, FEAT), BF16), dma((3,)), dma((3,)),
        ],
        name="put",
    )(*found)


def solution(mesh):
    return jax.shard_map(
        per_device,
        mesh=mesh,
        in_specs=(
            P("ctx", None),
            P("ctx", None),
            P(),
            P(None, "hd"),
            P("hd", None),
            P("hd", "ctx"),
            P("ctx", "hd"),
            P("ctx", "hd"),
            P("ctx", "hd"),
            P(),
            P(),
        ),
        out_specs=(P("ctx", "hd"), P("ctx", "hd"), P("ctx", "hd")),
        check_vma=False,
    )
```

```python
import jax
import jax.numpy as jnp
from jax import lax
from jax.experimental import pallas as pl
from jax.experimental.pallas import tpu as pltpu
from jax.sharding import PartitionSpec as P

F32, BF16 = jnp.float32, jnp.bfloat16
MESH = pl.DeviceIdType.MESH
D = 1024
HID = 1024
FEAT = 256
HDIM = 64
HEADS = 4
EV = 256
LAT = 512
CTX_COUNT = 128
FIRST_EVENTS = 63
WIDE = 384
REST = 640
LATE = 32
EMPTY = -1e29
NN = (((1,), (0,)), ((), ()))
NT = (((1,), (1,)), ((), ()))


def gelu_slope(t):
    inner = 0.7978845608028654 * (t + 0.044715 * t * t * t)
    tangent = jnp.tanh(inner)
    return 0.5 * (1.0 + tangent) + 0.5 * t * (
        1.0 - tangent * tangent
    ) * 0.7978845608028654 * (1.0 + 0.134145 * t * t)


def dot(a, b, dims=NN):
    return lax.dot_general(a, b, dims, preferred_element_type=F32)


def pieces(stats):
    high = stats.astype(BF16).astype(F32)
    rest = stats - high
    middle = rest.astype(BF16).astype(F32)
    return high, middle, rest - middle


def lanes_of(rows, columns, offset):
    lane = lax.broadcasted_iota(jnp.int32, (rows, columns), 0) - offset
    to = lax.broadcasted_iota(jnp.int32, (rows, columns), 1)
    same = ((lane & 3) == ((to >> 6) & 3)) & (((lane >> 2) & 1) == (to >> 8))
    return jnp.where(same & (lane >= 0) & (lane < 24), 1.0, 0.0).astype(BF16)


def wide_rows(main, stats, offset):
    tail = [jnp.zeros((offset, LAT), F32)] if offset else []
    tail += [*pieces(stats), jnp.zeros((WIDE - FEAT - 24 - offset, LAT), F32)]
    return jnp.concatenate([main, *tail], axis=0).T.reshape(32, 16, WIDE)


def shares(tops, totals):
    top = tops[0]
    for n in range(1, len(tops)):
        top = jnp.maximum(top, tops[n])
    parts = [total * jnp.exp(own - top) for own, total in zip(tops, totals)]
    whole = parts[0]
    for n in range(1, len(tops)):
        whole = whole + parts[n]
    scale = jnp.where(whole > 0.0, 1.0 / whole, 0.0)
    return top, whole, [part * scale for part in parts]


def added(terms):
    whole = terms[0]
    for term in terms[1:]:
        whole = whole + term
    return whole


def kernel(
    cot_h, res_h, gain_h, win_h, wout_h, wt_h, q_h, k_h, v_h, pos_h, start_h,
    oq_v, dk_v, dv_v,
    cot_v, res_v, gain_v, win_v, wout_v, wslab, q_v, kbuf, vbuf, pos_v,
    part_s, hdbuf, zw, wfull, qz, qblk, qbuf, rgz, rgall, dosend, dobuf,
    kmask, vmask, kt, bias, pown, gown, near_s, near_r,
    rest_s, rest_r, first_s, first_r, early_zs, early_zr, late_zs, late_zr,
    lsem, ssem, hd_sem, zw_sem, qz_sem, near_sem, w_sem, q_sem, rgz_sem, rgp_sem,
    do_sem, rest_sem, first_sem, early_z_sem, late_z_sem,
):
    c = lax.axis_index("ctx")
    hd = lax.axis_index("hd")
    core = c % 2
    x = (c // 2) % 4
    zh = (c // 8) % 4
    y = c // 32
    chip = y * 4 + x
    slot = chip * 2 + core
    active = y >= 2
    edge = c == FIRST_EVENTS
    takes_part = c >= FIRST_EVENTS

    def ctx_of(y_, zh_, x_, core_):
        return ((y_ * 4 + zh_) * 4 + x_) * 2 + core_

    barrier = pltpu.get_barrier_semaphore()
    greeted = []
    for d in (4, 5, 2, 3, 6, 7, 1):
        other = (zh * 2 + core + d) % 8
        greeted.append((ctx_of(y, other // 2, x, other % 2), hd))
    for d in range(1, 4):
        greeted.append((c, (hd + d) % 4))
    greeted.append(((c + 1) % CTX_COUNT, hd))
    greeted.append(((c + CTX_COUNT - 1) % CTX_COUNT, hd))
    for d in range(1, 32):
        other = (slot + d) % 32
        greeted.append((ctx_of(other // 8, zh, (other // 2) % 4, other % 2), hd))
    for who in greeted:
        pl.semaphore_signal(barrier, inc=1, device_id=who, device_id_type=MESH)

    loads = {}

    def load(name, src, dst, k):
        copy = pltpu.make_async_copy(src, dst, lsem.at[k])
        copy.start()
        loads[name] = copy

    load("res", res_h, res_v, 0)
    load("cot", cot_h, cot_v, 1)
    load("gain", gain_h, gain_v, 2)
    for n in range(4):
        load(f"win{n}", win_h.at[pl.ds(256 * n, 256)], win_v.at[pl.ds(256 * n, 256)], 3 + n)
    for n in range(4):
        load(f"wout{n}", wout_h.at[pl.ds(256 * n, 256)], wout_v.at[pl.ds(256 * n, 256)], 7 + n)
    load("wt", wt_h, wslab, 11)
    load("q", q_h, q_v, 12)
    load("k", k_h, kbuf, 13)
    load("v", v_h, vbuf, 14)
    load("start", start_h, pos_v.at[0], 15)
    load("pos", pos_h, pos_v.at[1], 16)

    def send(src, dst, send_sem, recv_sem, who, cond=None):
        copy = pltpu.make_async_remote_copy(
            src_ref=src, dst_ref=dst, send_sem=send_sem, recv_sem=recv_sem,
            device_id=who, device_id_type=MESH,
        )
        if cond is None:
            copy.start()
        else:
            pl.when(cond)(copy.start)

    def arrived(ref, sem):
        pltpu.make_async_copy(ref, ref, sem).wait()

    loads["res"].wait()
    loads["gain"].wait()
    loads["cot"].wait()
    rows = res_v[...].astype(F32)
    inv_rms = lax.rsqrt(jnp.mean(rows * rows, axis=-1, keepdims=True) + 1e-05)
    gain_rows = gain_v[...].astype(F32)
    gain = jnp.concatenate([gain_rows[n : n + 1, :] for n in range(8)], axis=1)
    normed = (rows * inv_rms * gain).astype(BF16)
    cot = cot_v[...]
    pre = jnp.zeros((4, HID), F32)
    for n in range(4):
        loads[f"win{n}"].wait()
        pre = pre + dot(normed[:, 256 * n : 256 * n + 256], win_v[256 * n : 256 * n + 256, :])
    slope = gelu_slope(pre)
    hidden = []
    for n in range(4):
        loads[f"wout{n}"].wait()
        hidden.append(dot(cot, wout_v[256 * n : 256 * n + 256, :], NT))
    pre_grad = (jnp.concatenate(hidden, axis=1) * slope).astype(BF16)
    part = dot(pre_grad, win_v[...], NT)
    part_s[...] = part

    loads["wt"].wait()
    loads["q"].wait()
    loads["k"].wait()
    loads["v"].wait()
    loads["pos"].wait()
    loads["start"].wait()
    pl.semaphore_wait(barrier, len(greeted))

    for d in range(1, 4):
        send(part_s, hdbuf.at[hd], ssem.at[0], hd_sem, (c, (hd + d) % 4))
    for d in range(1, 8):
        other = (zh * 2 + core + d) % 8
        send(
            wslab.at[other % 2], zw.at[zh * 2 + core], ssem.at[1], zw_sem,
            (ctx_of(y, other // 2, x, other % 2), hd),
        )
    for d in range(1, 4):
        send(q_v, qz.at[zh], ssem.at[2], qz_sem, (ctx_of(y, (zh + d) % 4, x, core), hd))
    hdbuf[hd] = part
    zw[zh * 2 + core] = wslab[core]
    qz[zh] = q_v[...]

    @pl.when(jnp.logical_not(takes_part))
    def _():
        dk_v[...] = jnp.zeros_like(dk_v)
        dv_v[...] = jnp.zeros_like(dv_v)

    @pl.when(takes_part)
    def _():
        base = c * EV
        spots = jnp.concatenate([pos_v[0], pos_v[1]], axis=0) - base
        to = lax.broadcasted_iota(jnp.int32, (128, 128), 1)
        origin = ((to >> 2) & 3) * 32 + (to >> 5) * 8 + ((to >> 4) & 1) * 4 + (to & 3)
        pick = jnp.where(lax.broadcasted_iota(jnp.int32, (128, 128), 0) == origin, 1.0, 0.0)
        moved = lax.dot_general(
            spots.astype(F32), pick, NN,
            precision=lax.Precision.HIGHEST, preferred_element_type=F32,
        )
        start = jnp.concatenate([moved[n : n + 1, :] for n in range(4)], axis=1)
        stop = jnp.concatenate([moved[n : n + 1, :] for n in range(4, 8)], axis=1)
        event = lax.broadcasted_iota(jnp.int32, (EV, LAT), 0).astype(F32)
        seen = (event >= start) & (event <= stop)
        bias[...] = jnp.where(seen, 0.0, -1e30)
        lane_head = lax.broadcasted_iota(jnp.int32, (1, FEAT), 1) // HDIM
        keys = kbuf[...].astype(F32) * 0.125
        values = vbuf[...].astype(F32)
        kt[...] = keys.T.astype(BF16)
        for h in range(HEADS):
            kmask[h] = jnp.where(lane_head == h, keys, 0.0).astype(BF16)
            vmask[h] = jnp.where(lane_head == h, values, 0.0).astype(BF16)

    arrived(hdbuf.at[0:3], hd_sem)
    normed_grad = (hdbuf[0] + hdbuf[1]) + (hdbuf[2] + hdbuf[3])
    weighted = normed_grad * gain
    unit = rows * inv_rms
    resid_grad = (
        cot.astype(F32)
        + inv_rms * (weighted - unit * jnp.mean(weighted * unit, axis=-1, keepdims=True))
    ).astype(BF16)
    rgz[zh] = resid_grad
    for d in range(1, 4):
        send(rgz.at[zh], rgz.at[zh], ssem.at[3], rgz_sem, (ctx_of(y, (zh + d) % 4, x, core), hd))

    arrived(zw.at[0:7], zw_sem)
    for j in range(4):
        both = jnp.concatenate([zw[2 * j].astype(F32), zw[2 * j + 1].astype(F32)], axis=0)
        wfull[y, j, x] = both.astype(BF16)
    for d in range(1, 16):
        other = (chip + d) % 16
        send(
            wfull.at[y, :, x], wfull.at[y, :, x], ssem.at[4], w_sem,
            (ctx_of(other // 4, zh, other % 4, core), hd),
        )

    arrived(qz.at[0:3], qz_sem)
    qblk[...] = jnp.concatenate([qz[j].astype(F32) for j in range(4)], axis=0).astype(BF16)

    def to_holders(src, dst, send_sem, sem):
        for d in range(16):
            t = (slot + d) % 16
            who = ctx_of(2 + t // 8, zh, (t // 2) % 4, t % 2)
            send(src, dst, send_sem, sem, (who, hd), who != c)
        send(src, dst, send_sem, sem, (FIRST_EVENTS, hd), (zh == 3) & (c != FIRST_EVENTS))

    others = 16 - jnp.where(active, 1, 0) + jnp.where((zh == 3) & (c != FIRST_EVENTS), 1, 0)

    def counted(buf, sem):
        for n in (15, 16, 17):
            pl.when(others == n)(lambda: arrived(buf.at[0:n], sem))

    to_holders(qblk, qbuf.at[slot], ssem.at[5], q_sem)

    arrived(rgz.at[0:3], rgz_sem)
    rgall[core] = jnp.concatenate([rgz[j].astype(F32) for j in range(4)], axis=0).astype(BF16)
    send(rgall.at[core], rgall.at[core], ssem.at[6], rgp_sem, (ctx_of(y, zh, x, 1 - core), hd))

    @pl.when(takes_part)
    def _():
        qbuf[slot] = qblk[...]

    arrived(dobuf.at[0:30], w_sem)
    arrived(rgall.at[1 - core], rgp_sem)
    out_half = dot(rgall[...].reshape(32, D), wfull[...].reshape(D, 128)).astype(BF16)
    dosend[...] = out_half
    to_holders(dosend, dobuf.at[core * 16 + chip], ssem.at[7], do_sem)

    @pl.when(takes_part)
    def _():
        dobuf[core * 16 + chip] = dosend[...]

    @pl.when(takes_part)
    def _():
        arrived(qbuf.at[0:31], q_sem)

    @pl.when(takes_part)
    def _():
        tops, totals, mixed = [], [], []
        for h in range(HEADS):
            scores = dot(kmask[h], qbuf[...].reshape(LAT, FEAT), NT) + bias[...]
            top = jnp.maximum(jnp.max(scores, axis=0, keepdims=True), EMPTY)
            expo = jnp.exp(scores - top)
            total = jnp.sum(expo, axis=0, keepdims=True)
            probs = expo * jnp.where(total > 0.0, 1.0 / total, 0.0)
            pown[h] = probs
            mixed.append(dot(kt[h * HDIM : (h + 1) * HDIM, :], probs.astype(BF16)))
            tops.append(top)
            totals.append(total)
        stats = jnp.concatenate(tops + totals, axis=0)
        near_s[0:8, :] = stats
        wide = wide_rows(jnp.concatenate(mixed, axis=0), stats, 0)
        for n in range(2):
            first_s[n] = wide[:, 4 * n : 4 * n + 4, :].astype(BF16)
        rest_s[:, :, FEAT:] = wide[:, 8:, :].astype(BF16)

    my_turn = jnp.where(active, (y - 2) * 8 + x * 2 + core, 16)

    def to_owners(src, dst, send_sem, sem):
        for d in range(1, 32):
            s = (slot + d) % 32
            send(
                src.at[s], dst.at[my_turn], send_sem, sem,
                (ctx_of(s // 8, zh, (s // 2) % 4, s % 2), hd), takes_part,
            )

    for n in range(2):
        to_owners(first_s.at[n], first_r.at[n], ssem.at[8 + n], first_sem.at[n])

    @pl.when(takes_part)
    def _():
        for n in range(2):
            first_r[n, my_turn] = first_s[n, slot]

    @pl.when(zh != 3)
    def _():
        lane = lax.broadcasted_iota(jnp.int32, (8, WIDE), 1)
        nobody = jnp.where((lane >> 2) == (FEAT >> 2), EMPTY, 0.0)
        for n in range(2):
            first_r[n, 16] = nobody[0:4, :].astype(BF16)
            first_r[2 + n, 16] = jnp.zeros((4, WIDE), BF16)
        rest_r[16, :, 0:FEAT] = jnp.zeros((8, FEAT), BF16)
        rest_r[16, :, FEAT:] = nobody.astype(BF16)

    @pl.when(takes_part)
    def _():
        arrived(dobuf.at[0:31], do_sem)

    def all_grads():
        return jnp.concatenate(
            [dobuf[0:16].reshape(LAT, 128), dobuf[16:32].reshape(LAT, 128)], axis=1
        )

    @pl.when(takes_part)
    def _():
        grads_t = all_grads().astype(F32).T.astype(BF16)
        deltas, mixed = [], []
        for h in range(HEADS):
            prob_grad = dot(vmask[h], grads_t)
            gown[h] = prob_grad
            probs = pown[h]
            delta = jnp.sum(probs * prob_grad, axis=0, keepdims=True)
            score_grad = (probs * (prob_grad - delta)).astype(BF16)
            mixed.append(dot(kt[h * HDIM : (h + 1) * HDIM, :], score_grad))
            deltas.append(delta)
        stats = jnp.concatenate(deltas + [jnp.zeros((4, LAT), F32)], axis=0)
        near_s[8:16, :] = stats
        wide = wide_rows(jnp.concatenate(mixed, axis=0), stats, LATE)
        for n in range(2):
            first_s[2 + n] = wide[:, 4 * n : 4 * n + 4, :].astype(BF16)
        rest_s[:, :, 0:FEAT] = wide[:, 8:, 0:FEAT].astype(BF16)
        tails = rest_s[:, :, 2 * FEAT :].astype(F32) + wide[:, 8:, FEAT:]
        rest_s[:, :, 2 * FEAT :] = tails.astype(BF16)

    for n in range(2, 4):
        to_owners(first_s.at[n], first_r.at[n], ssem.at[12 + n], first_sem.at[n])
    to_owners(rest_s, rest_r, ssem.at[16], rest_sem)
    up = takes_part & (c < CTX_COUNT - 1)
    down = c > FIRST_EVENTS
    send(near_s, near_r.at[0], ssem.at[10], near_sem.at[0], ((c + 1) % CTX_COUNT, hd), up)
    send(near_s, near_r.at[1], ssem.at[11], near_sem.at[1], ((c + CTX_COUNT - 1) % CTX_COUNT, hd), down)

    @pl.when(takes_part)
    def _():
        for n in range(2, 4):
            first_r[n, my_turn] = first_s[n, slot]
        rest_r[my_turn] = rest_s[slot]

    def split_early(held):
        rows = held[0].shape[0]
        tails = jnp.concatenate([one[:, FEAT:] for one in held], axis=0).astype(BF16)
        spread = dot(tails, lanes_of(WIDE - FEAT, 2 * FEAT, 0))
        tops = [spread[rows * n : rows * n + rows, 0:FEAT] for n in range(17)]
        totals = [spread[rows * n : rows * n + rows, FEAT:] for n in range(17)]
        top, whole, weights = shares(tops, totals)
        mean_keys = [one[:, 0:FEAT] for one in held]
        return top, whole, weights, mean_keys, added([w * k for w, k in zip(weights, mean_keys)])

    def merge_late(held, weights, mean_keys):
        rows = held[0].shape[0]
        tails = jnp.concatenate([one[:, FEAT:] for one in held], axis=0).astype(BF16)
        spread = dot(tails, lanes_of(WIDE - FEAT, FEAT, LATE))
        deltas = [spread[rows * n : rows * n + rows, :] for n in range(17)]
        delta = added([w * own for w, own in zip(weights, deltas)])
        merged = added([
            w * (one[:, 0:FEAT] - (delta - own) * mean)
            for w, one, own, mean in zip(weights, held, deltas, mean_keys)
        ])
        lane = lax.broadcasted_iota(jnp.int32, (FEAT, WIDE - FEAT), 0)
        to = lax.broadcasted_iota(jnp.int32, (FEAT, WIDE - FEAT), 1)
        compact = added([
            dot(
                piece.astype(BF16),
                jnp.where(((lane & 63) == 0) & (to == k * 8 + (lane >> 6)), 1.0, 0.0).astype(BF16),
            )
            for k, piece in enumerate(pieces(delta))
        ])
        return merged, compact

    def keep_early(j, rows, found):
        for k, part_ in enumerate(found):
            early_zs[j, :, k * FEAT : (k + 1) * FEAT] = part_[rows : rows + 4, :]

    def keep_late(j, rows, merged, compact):
        late_zs[j, :, 0:FEAT] = merged[rows : rows + 4, :].astype(BF16)
        late_zs[j, :, FEAT:] = compact[rows : rows + 4, :].astype(BF16)

    def along_z(src, dst, send_sem, sem, targets):
        for j in targets:
            send(src.at[j], dst.at[zh], send_sem, sem, (ctx_of(y, j, x, core), hd), zh != j)

    kept = []
    for n in range(2):
        counted(first_r.at[n], first_sem.at[n])
        held = [first_r[n, t].astype(F32) for t in range(17)]
        top, whole, weights, mean_keys, mean_key = split_early(held)
        keep_early(n, 0, (top, whole, mean_key))
        along_z(early_zs, early_zr, ssem.at[12], early_z_sem, (n,))
        kept.append((weights, mean_keys))
    for n in range(2):
        counted(first_r.at[2 + n], first_sem.at[2 + n])
        held = [first_r[2 + n, t].astype(F32) for t in range(17)]
        keep_late(n, 0, *merge_late(held, *kept[n]))
        along_z(late_zs, late_zr, ssem.at[13], late_z_sem, (n,))

    counted(rest_r, rest_sem)
    held = [rest_r[t].astype(F32) for t in range(17)]
    top, whole, weights, mean_keys, mean_key = split_early([one[:, FEAT:] for one in held])
    merged, compact = merge_late(
        [jnp.concatenate([one[:, 0:FEAT], one[:, 2 * FEAT :]], axis=1) for one in held],
        weights, mean_keys,
    )
    for j in range(2, 4):
        keep_early(j, 4 * (j - 2), (top, whole, mean_key))
        keep_late(j, 4 * (j - 2), merged, compact)
    along_z(late_zs, late_zr, ssem.at[13], late_z_sem, (2, 3))
    along_z(early_zs, early_zr, ssem.at[12], early_z_sem, (2, 3))
    early_zr[zh] = early_zs[zh]
    late_zr[zh] = late_zs[zh]

    @pl.when(takes_part)
    def _():
        nothing = jnp.concatenate(
            [jnp.full((4, LAT), EMPTY, F32), jnp.zeros((12, LAT), F32)], axis=0
        )

        @pl.when(c == FIRST_EVENTS)
        def _():
            near_r[0] = nothing

        @pl.when(c == CTX_COUNT - 1)
        def _():
            near_r[1] = nothing

        @pl.when(c > FIRST_EVENTS)
        def _():
            arrived(near_r.at[0], near_sem.at[0])

        @pl.when(c < CTX_COUNT - 1)
        def _():
            arrived(near_r.at[1], near_sem.at[1])

    @pl.when(takes_part)
    def _():
        three = (near_s[...], near_r[0], near_r[1])
        unused_top, unused_whole, parts = shares(
            [one[0:4, :] for one in three], [one[4:8, :] for one in three]
        )
        delta = added([w * one[8:12, :] for w, one in zip(parts, three)])
        queries = qbuf[...].reshape(LAT, FEAT)
        grads = all_grads()
        lane_head = lax.broadcasted_iota(jnp.int32, (1, FEAT), 1) // HDIM
        dk = jnp.zeros((EV, FEAT), F32)
        dv = jnp.zeros((EV, FEAT), F32)
        for h in range(HEADS):
            probs = pown[h] * parts[0][h : h + 1, :]
            score_grad = (probs * (gown[h] - delta[h : h + 1, :])).astype(BF16)
            dk = jnp.where(lane_head == h, dot(score_grad, queries), dk)
            dv = jnp.where(lane_head == h, dot(probs.astype(BF16), grads), dv)
        dk_v[...] = (dk * 0.125).astype(BF16)
        dv_v[...] = dv.astype(BF16)

    arrived(early_zr.at[0:3], early_z_sem)
    tops = [early_zr[j][:, 0:FEAT] for j in range(4)]
    totals = [early_zr[j][:, FEAT : 2 * FEAT] for j in range(4)]
    mean_keys = [early_zr[j][:, 2 * FEAT :] for j in range(4)]
    unused_top, unused_whole, weights = shares(tops, totals)
    arrived(late_zr.at[0:3], late_z_sem)
    late = [late_zr[j].astype(F32) for j in range(4)]
    spread = dot(
        jnp.concatenate([one[:, FEAT:] for one in late], axis=0).astype(BF16),
        lanes_of(WIDE - FEAT, FEAT, 0),
    )
    deltas = [spread[4 * j : 4 * j + 4, :] for j in range(4)]
    delta = added([w * own for w, own in zip(weights, deltas)])
    total = added([
        weights[j] * (late[j][:, 0:FEAT] - (delta - deltas[j]) * mean_keys[j]) for j in range(4)
    ])
    oq_v[...] = total.astype(BF16)
    arrived(hdbuf.at[0:3], ssem.at[0])
    arrived(zw.at[0:7], ssem.at[1])
    arrived(qz.at[0:3], ssem.at[2])
    arrived(rgz.at[0:3], ssem.at[3])
    arrived(dobuf.at[0:30], ssem.at[4])
    counted(qbuf, ssem.at[5])
    arrived(rgall.at[0], ssem.at[6])
    counted(dobuf, ssem.at[7])

    @pl.when(takes_part)
    def _():
        for n in range(2):
            arrived(first_s.at[n, 0:31], ssem.at[8 + n])
            arrived(first_s.at[2 + n, 0:31], ssem.at[14 + n])
        arrived(rest_s.at[0:31], ssem.at[16])

    @pl.when(up)
    def _():
        arrived(near_s, ssem.at[10])

    @pl.when(down)
    def _():
        arrived(near_s, ssem.at[11])

    arrived(early_zr.at[0:3], ssem.at[12])
    arrived(late_zr.at[0:3], ssem.at[13])


def put(q_in, k_in, v_in, q_out, k_out, v_out, sem):
    copies = [
        pltpu.make_async_copy(src, dst, sem.at[n])
        for n, (src, dst) in enumerate(((k_in, k_out), (v_in, v_out), (q_in, q_out)))
    ]
    for copy in copies:
        copy.start()
    for copy in copies:
        copy.wait()


def per_device(
    cot, resid, norm_gain, w_in, w_out, w_proj, queries, keys, values, latent_pos, seg_start
):
    w_halves = w_proj.reshape(2, 128, 8).transpose(0, 2, 1)
    anywhere = pl.BlockSpec(memory_space=pl.ANY)
    dma = pltpu.SemaphoreType.DMA
    vm = pltpu.VMEM
    shapes = (
        jax.ShapeDtypeStruct((4, FEAT), BF16),
        jax.ShapeDtypeStruct((EV, FEAT), BF16),
        jax.ShapeDtypeStruct((EV, FEAT), BF16),
    )
    found = pl.pallas_call(
        kernel,
        out_shape=tuple(vm(one.shape, BF16) for one in shapes),
        in_specs=[anywhere] * 11,
        out_specs=(pl.BlockSpec(memory_space=vm),) * 3,
        scratch_shapes=[
            vm((4, D), BF16),
            vm((4, D), BF16),
            vm((8, 128), BF16),
            vm((D, HID), BF16),
            vm((HID, D), BF16),
            vm((2, 8, 128), BF16),
            vm((4, FEAT), BF16),
            vm((EV, FEAT), BF16),
            vm((EV, FEAT), BF16),
            vm((2, 4, 128), jnp.int32),
            vm((4, D), F32),
            vm((4, 4, D), F32),
            vm((8, 8, 128), BF16),
            vm((4, 4, 4, 16, 128), BF16),
            vm((4, 4, FEAT), BF16),
            vm((16, FEAT), BF16),
            vm((32, 16, FEAT), BF16),
            vm((4, 4, D), BF16),
            vm((2, 16, D), BF16),
            vm((32, 128), BF16),
            vm((32, 32, 128), BF16),
            vm((HEADS, EV, FEAT), BF16),
            vm((HEADS, EV, FEAT), BF16),
            vm((FEAT, EV), BF16),
            vm((EV, LAT), F32),
            vm((HEADS, EV, LAT), F32),
            vm((HEADS, EV, LAT), F32),
            vm((16, LAT), F32),
            vm((2, 16, LAT), F32),
            vm((32, 8, REST), BF16),
            vm((17, 8, REST), BF16),
            vm((4, 32, 4, WIDE), BF16),
            vm((4, 17, 4, WIDE), BF16),
            vm((4, 4, 3 * FEAT), F32),
            vm((4, 4, 3 * FEAT), F32),
            vm((4, 4, WIDE), BF16),
            vm((4, 4, WIDE), BF16),
            dma((17,)),
            dma((17,)),
            dma, dma, dma,
            dma((2,)),
            dma, dma, dma, dma, dma, dma,
            dma((4,)),
            dma, dma,
        ],
        compiler_params=pltpu.CompilerParams(collective_id=0, has_side_effects=True),
        name="backward",
    )(
        cot, resid, norm_gain.reshape(8, 128), w_in, w_out, w_halves, queries, keys, values,
        latent_pos.reshape(4, 128), seg_start.reshape(4, 128),
    )
    return pl.pallas_call(
        put,
        out_shape=shapes,
        in_specs=[anywhere] * 3,
        out_specs=(anywhere,) * 3,
        scratch_shapes=[dma((3,))],
        name="put",
    )(*(pltpu.with_memory_space_constraint(one, vm) for one in found))


def solution(mesh):
    return jax.shard_map(
        per_device,
        mesh=mesh,
        in_specs=(
            P("ctx", None),
            P("ctx", None),
            P(),
            P(None, "hd"),
            P("hd", None),
            P("hd", "ctx"),
            P("ctx", "hd"),
            P("ctx", "hd"),
            P("ctx", "hd"),
            P(),
            P(),
        ),
        out_specs=(P("ctx", "hd"), P("ctx", "hd"), P("ctx", "hd")),
        check_vma=False,
    )
```
